256 devices in a mesh: dp: 64 (over z_hi, x, y, core), own: 4 (over z_lo).
Axes of the slice: x: 4, y: 4, z: 8 (z_hi: 2, z_lo: 4; z = z_hi * 4 + z_lo), core: 2. Of those that a mesh axis runs over, the one named last changes fastest.
Arguments:
- acts_q: bfloat16 [262144, 512], P(('dp', 'own')), may hold values from -54 to 54
- grads_q: bfloat16 [262144, 384], P(('dp', 'own')), may hold values from -180 to 180
- acts_o: bfloat16 [262144, 384], P(('dp', 'own')), may hold values from -54 to 54
- grads_o: bfloat16 [262144, 512], P(('dp', 'own')), may hold values from -180 to 180
- sample_rows: int32 [4096], P(('dp', 'own')), may hold values from 0 to 1023
- start_aq: float32 [512, 512], replicated, may hold values from -2 to 16, as said below
- start_gq: float32 [384, 384], replicated, may hold values from -2 to 16, as said below
- start_ao: float32 [384, 384], replicated, may hold values from -2 to 16, as said below
- start_go: float32 [512, 512], replicated, may hold values from -2 to 16, as said below
- weight_q: float32 [512, 384], P('dp', 'own'), may hold values from -0.25 to 0.25
- weight_o: float32 [384, 512], P('dp', 'own'), may hold values from -0.3125 to 0.3125
Outputs:
- new_q: float32 [512, 384], replicated
- new_o: float32 [384, 512], replicated
The draws below stay inside these ranges and needn't reach their ends.
Inputs may be any that keep to these rules, and one draw needn't show every extreme that they name: `start_aq`: symmetric positive definite. `start_gq`: symmetric positive definite. `start_ao`: symmetric positive definite. `start_go`: symmetric positive definite.
All inputs are finite; a program needn't handle non-finite values.
Results may differ from the reference program's by a relative error of at most 0.0008.
Values may be sent and summed in bfloat16 or wider, within the bound.
A program may use at most 128 MiB of HBM per device.

```python
import math
import jax
import jax.numpy as jnp
from jax import lax

D = 512
INNER = 384
TOK_DEV = 1024
SAMPLE_DEV = 16
ITERS = 4
TOKENS = 262144
SAMPLES = 4096


def log_spread(subkey, shape, low, high):
    return jnp.exp(jax.random.uniform(subkey, shape, jnp.float32, math.log(low), math.log(high)))


def token_pair(base_key, salt, width_in, width_out):
    subkeys = [jax.random.fold_in(jax.random.fold_in(base_key, salt), index) for index in range(6)]
    row_scale = log_spread(subkeys[0], (TOKENS, 1), 0.3, 3.0)
    noise_in = jnp.clip(jax.random.normal(subkeys[1], (TOKENS, width_in), jnp.float32), -6.0, 6.0)
    noise_out = jnp.clip(jax.random.normal(subkeys[4], (TOKENS, width_out), jnp.float32), -6.0, 6.0)
    col_in = log_spread(subkeys[2], (1, width_in), 0.3, 3.0)
    activations = noise_in * row_scale * col_in
    half_width = math.sqrt(3.0 / width_in)
    mixing = jax.random.uniform(subkeys[3], (width_in, width_out), jnp.float32, -half_width, half_width)
    source = jnp.dot(activations, mixing, precision=lax.Precision.HIGHEST)
    col_out = log_spread(subkeys[5], (1, width_out), 0.3, 3.0)
    gradients = jnp.clip(col_out * (source + noise_out), -180.0, 180.0)
    return (activations, gradients)


def start_factor(base_key, salt, width):
    first = jax.random.fold_in(jax.random.fold_in(base_key, salt), 1)
    second = jax.random.fold_in(jax.random.fold_in(base_key, salt), 2)
    scales = jnp.sqrt(log_spread(first, (width,), 1.0, 10.0))
    half_range = 0.433 / math.sqrt(width)
    raw = jax.random.uniform(second, (width, width), jnp.float32, -half_range, half_range)
    identity = jnp.eye(width, dtype=jnp.float32)
    symmetric = (raw + raw.T) * 0.70710678
    core = symmetric * (1.0 - identity) + identity
    return scales[:, None] * core * scales[None, :]


def draw_acts_q(key, part):
    return token_pair(key, 11, D, INNER)[0].astype(jnp.bfloat16)


def draw_grads_q(key, part):
    return token_pair(key, 11, D, INNER)[1].astype(jnp.bfloat16)


def draw_acts_o(key, part):
    return token_pair(key, 12, INNER, D)[0].astype(jnp.bfloat16)


def draw_grads_o(key, part):
    return token_pair(key, 12, INNER, D)[1].astype(jnp.bfloat16)


def draw_start_aq(key, part):
    return start_factor(key, 21, D)


def draw_start_gq(key, part):
    return start_factor(key, 22, INNER)


def draw_start_ao(key, part):
    return start_factor(key, 23, INNER)


def draw_start_go(key, part):
    return start_factor(key, 24, D)


def plant(drawn, own_key, least, high):
    index_at = [jax.random.randint(jax.random.fold_in(own_key, axis), (), 0, length) for axis, length in enumerate(drawn.shape)]
    widest = drawn.shape.index(max(drawn.shape))
    neighbour = index_at[:widest] + [(index_at[widest] + 1) % drawn.shape[widest]] + index_at[widest + 1:]
    return drawn.at[tuple(index_at)].set(least).at[tuple(neighbour)].set(high)


def steps_of(rng, shape, pieces, low, largest):
    gain = 1.0
    for position, parts in pieces:
        steps = jax.random.uniform(jax.random.fold_in(jax.random.fold_in(rng, 6), position), (parts,), jnp.float32, low / len(pieces), largest / len(pieces))
        gain = gain * jnp.repeat(jnp.exp(steps), shape[position] // parts).reshape((-1,) + (1,) * (len(shape) - 1 - position))
    return gain


def noise(stream_key, shape, scale, most, split=(), kind=jnp.bfloat16):
    array = jax.random.normal(stream_key, shape, jnp.float32) * scale
    if len(split) > 0:
        array = steps_of(stream_key, shape, split, -0.22, 0.18) * array
    return jnp.clip(array, min=-most, max=most).astype(kind)


def setup_inputs(seed: int = 0) -> dict:
    streams_of = jax.random.split(jax.random.key(seed), 12)
    return {
        "acts_q": draw_acts_q(jax.random.fold_in(streams_of[11], 71), 0),
        "grads_q": draw_grads_q(jax.random.fold_in(streams_of[11], 71), 0),
        "acts_o": draw_acts_o(jax.random.fold_in(streams_of[11], 71), 0),
        "grads_o": draw_grads_o(jax.random.fold_in(streams_of[11], 71), 0),
        "sample_rows": plant(jax.random.randint(streams_of[4], (SAMPLES,), 0, TOK_DEV), jax.random.fold_in(streams_of[4], 1), 0, TOK_DEV - 1).astype(jnp.int32),
        "start_aq": draw_start_aq(jax.random.fold_in(streams_of[11], 71), 0),
        "start_gq": draw_start_gq(jax.random.fold_in(streams_of[11], 71), 0),
        "start_ao": draw_start_ao(jax.random.fold_in(streams_of[11], 71), 0),
        "start_go": draw_start_go(jax.random.fold_in(streams_of[11], 71), 0),
        "weight_q": noise(streams_of[9], (D, INNER), D ** -0.5, 0.25, ((0, 64), (1, 4)), jnp.float32),
        "weight_o": noise(streams_of[10], (INNER, D), INNER ** -0.5, 0.3125, ((0, 64), (1, 4)), jnp.float32),
    }


DECAY = 0.5
DAMPING = 0.5
LEARNING_RATE = 10.0

def damped(start, cov):
    width = start.shape[0]
    return DECAY * start + (1.0 - DECAY) * cov + DAMPING * jnp.eye(width, dtype=jnp.float32)

def newton(matrix):
    width = matrix.shape[0]
    scale = 1.0 / jnp.sqrt(jnp.sum(matrix * matrix))
    approx = scale * jnp.eye(width, dtype=jnp.float32)
    for iteration in range(ITERS):
        product = jnp.dot(matrix, approx, precision=lax.Precision.HIGHEST)
        approx = 2.0 * approx - jnp.dot(product, approx, precision=lax.Precision.HIGHEST)
    return approx

def covariance(sampled):
    return jnp.dot(sampled.T, sampled, preferred_element_type=jnp.float32) / SAMPLES

def reference(acts_q, grads_q, acts_o, grads_o, sample_rows, start_aq, start_gq, start_ao, start_go, weight_q, weight_o):
    offsets = jnp.arange(SAMPLES, dtype=jnp.int32) // SAMPLE_DEV * TOK_DEV + sample_rows.astype(jnp.int32)
    inv_aq = newton(damped(start_aq, covariance(jnp.take(acts_q, offsets, axis=0))))
    inv_gq = newton(damped(start_gq, covariance(jnp.take(grads_q, offsets, axis=0))))
    inv_ao = newton(damped(start_ao, covariance(jnp.take(acts_o, offsets, axis=0))))
    inv_go = newton(damped(start_go, covariance(jnp.take(grads_o, offsets, axis=0))))
    grad_q = jnp.dot(acts_q.T, grads_q, preferred_element_type=jnp.float32) / TOKENS
    grad_o = jnp.dot(acts_o.T, grads_o, preferred_element_type=jnp.float32) / TOKENS
    left_q = jnp.dot(inv_aq, grad_q, precision=lax.Precision.HIGHEST)
    left_o = jnp.dot(inv_ao, grad_o, precision=lax.Precision.HIGHEST)
    new_q = weight_q - LEARNING_RATE * jnp.dot(left_q, inv_gq, precision=lax.Precision.HIGHEST)
    new_o = weight_o - LEARNING_RATE * jnp.dot(left_o, inv_go, precision=lax.Precision.HIGHEST)
    return (new_q, new_o)
```

```python
import functools

import jax
import jax.numpy as jnp
from jax import lax
from jax.experimental import pallas as pl
from jax.experimental.pallas import tpu as pltpu
from jax.sharding import PartitionSpec as P

MESH = pl.DeviceIdType.MESH
F32 = jnp.float32
BF16 = jnp.bfloat16
DECAY = 0.5
DAMPING = 0.5
LEARNING_RATE = 10.0
TOKENS = 262144
SAMPLES = 4096
BIG = 512
SMALL = 384
BLK = 128
PAIRS = [(i, j) for i in range(4) for j in range(i, 4)] + [
    (i, j) for i in range(4, 7) for j in range(i, 7)
]


def lookup(index, table):
    value = jnp.int32(table[0])
    for position in range(1, len(table)):
        value = jnp.where(index == position, jnp.int32(table[position]), value)
    return value


def dot(a, b, dims=((1,), (0,))):
    return lax.dot_general(a, b, (dims, ((), ())), preferred_element_type=F32)


def high_low(value):
    high = value.astype(BF16)
    return high, (value - high.astype(F32)).astype(BF16)


def dot3(a, b, dims=((1,), (0,))):
    return dot(a[0], b[0], dims) + dot(a[0], b[1], dims) + dot(a[1], b[0], dims)


def eye_mask(n):
    return lax.broadcasted_iota(jnp.int32, (n, n), 0) == lax.broadcasted_iota(
        jnp.int32, (n, n), 1
    )


def diagonal(ref, n):
    mask = eye_mask(BLK)
    cols, rows = [], []
    for i in range(n // BLK):
        at = slice(i * BLK, (i + 1) * BLK)
        block = jnp.where(mask, ref[at, at], 0.0)
        cols.append(jnp.sum(block, axis=1, keepdims=True))
        rows.append(jnp.sum(block, axis=0, keepdims=True))
    return cols, jnp.concatenate(rows, axis=1)


def row_eye(i, n):
    return lax.broadcasted_iota(jnp.int32, (BLK, n), 0) + i * BLK == lax.broadcasted_iota(
        jnp.int32, (BLK, n), 1
    )


def newton_step(n, e_ref, p_ref, eb_ref, pb_ref):
    blocks = range(n // BLK)
    e_col, e_row = diagonal(e_ref, n)
    for i in blocks:
        at = slice(i * BLK, (i + 1) * BLK)
        eb_ref[at, :] = jnp.where(row_eye(i, n), 0.0, e_ref[at, :]).astype(BF16)
        pb_ref[at, :] = jnp.where(row_eye(i, n), 0.0, p_ref[at, :]).astype(BF16)
    for i in blocks:
        at = slice(i * BLK, (i + 1) * BLK)
        square = dot(eb_ref[at, :], eb_ref[...])
        rest = e_ref[at, :]
        weight = jnp.where(row_eye(i, n), e_col[i], e_col[i] + e_row)
        e_ref[at, :] = square + weight * rest
    f_col, f_row = diagonal(e_ref, n)
    p_col, _ = diagonal(p_ref, n)
    for i in blocks:
        at = slice(i * BLK, (i + 1) * BLK)
        eb_ref[at, :] = jnp.where(row_eye(i, n), 0.0, e_ref[at, :]).astype(BF16)
    for i in blocks:
        at = slice(i * BLK, (i + 1) * BLK)
        product = dot(pb_ref[at, :], eb_ref[...])
        p_rows = p_ref[at, :]
        off = jnp.where(row_eye(i, n), 0.0, e_ref[at, :])
        p_ref[at, :] = p_rows + product + p_col[i] * off + p_rows * f_row


def kernel(
    acts_q, grads_q, acts_o, grads_o, rows_ref,
    start_aq, start_gq, start_ao, start_go, wq_ref, wo_ref,
    new_q, new_o,
    mine_b, mine_s, oth_b, oth_s, st_b, st_s,
    g_send, g_mine, g_core, g_y, g_ysum, g_x, g_xsum, g_z, g_full,
    s_send, s_core, s_all,
    c_part, c_y, c_ysum, c_z, c_blocks,
    w_send, w_all,
    e_b, p_b, eb_b, pb_b, e_s, p_s, eb_s, pb_s, m_ref,
    in_sem, send_sem, recv_sem,
):
    dp, own = lax.axis_index("dp"), lax.axis_index("own")
    core = lax.rem(dp, 2)
    y = lax.rem(dp // 2, 4)
    x = lax.rem(dp // 8, 4)
    z = (dp // 32) * 4 + own

    def device(cx, cy, cz, cc):
        return ((cz // 4) * 32 + cx * 8 + cy * 2 + cc, lax.rem(cz, 4))

    partner = device(x, y, z, 1 - core)
    x_peer = [device(lax.rem(x + d, 4), y, z, core) for d in range(4)]
    y_peer = [device(x, lax.rem(y + d, 4), z, core) for d in range(4)]
    z_peer = [device(x, y, lax.rem(z + d, 8), core) for d in range(8)]

    def fetch(src, dst, sem):
        return pltpu.make_async_copy(src, dst, in_sem.at[sem])

    @pl.when(core == 0)
    def _():
        fetch(acts_q, mine_b, 0).start()
        fetch(grads_q, mine_s, 1).start()
        fetch(grads_o, oth_b, 2).start()
        fetch(acts_o, oth_s, 3).start()
        fetch(start_aq, st_b, 4).start()
        fetch(start_gq, st_s, 5).start()

    @pl.when(core == 1)
    def _():
        fetch(grads_o, mine_b, 0).start()
        fetch(acts_o, mine_s, 1).start()
        fetch(acts_q, oth_b, 2).start()
        fetch(grads_q, oth_s, 3).start()
        fetch(start_go, st_b, 4).start()
        fetch(start_ao, st_s, 5).start()

    barrier = pltpu.get_barrier_semaphore()
    for peer in [partner] + x_peer[1:] + y_peer[1:] + z_peer[1:]:
        pl.semaphore_signal(barrier, inc=1, device_id=peer, device_id_type=MESH)

    def remote(src, dst, slot, peer):
        return pltpu.make_async_remote_copy(
            src_ref=src, dst_ref=dst, send_sem=send_sem.at[slot],
            recv_sem=recv_sem.at[slot], device_id=peer, device_id_type=MESH,
        )

    pending = []

    def send(src, dst, slot, peer):
        copy = remote(src, dst, slot, peer)
        copy.start()
        pending.append(copy)
        return copy

    w_send[...] = jnp.zeros_like(w_send)

    @pl.when(core == 0)
    def _():
        w_all[x, y, z, 0] = jnp.zeros((8, BLK), F32)
        w_all[x, y, z, 0, :, 0:96] = wq_ref[...]
        w_send[0:6, :] = wo_ref[...]

    @pl.when(core == 1)
    def _():
        w_all[x, y, z, 1] = jnp.zeros((8, BLK), F32)
        w_all[x, y, z, 1, 0:6, :] = wo_ref[...]
        w_send[:, 0:96] = wq_ref[...]

    fetch(acts_q, oth_b, 2).wait()
    fetch(grads_q, oth_s, 3).wait()
    fetch(acts_q, mine_b, 0).wait()
    fetch(grads_q, mine_s, 1).wait()

    target = jnp.zeros((16, 1024), jnp.int32)
    row = lax.broadcasted_iota(jnp.int32, (16, 1024), 0)
    for k in range(16):
        target = jnp.where(row == k, rows_ref[k], target)
    pick = lax.broadcasted_iota(jnp.int32, (16, 1024), 1) == target
    one_hot = jnp.where(pick, 1.0, 0.0).astype(BF16)

    def sampled(big, small):
        return jnp.concatenate([dot(one_hot, big[...]), dot(one_hot, small[...])], axis=1).astype(BF16)

    picked = sampled(oth_b, oth_s)
    for b in range(7):
        s_send[b] = picked[:, b * BLK : (b + 1) * BLK]
    picked = sampled(mine_b, mine_s)
    for b in range(7):
        s_all[x, b, pl.ds(pl.multiple_of(core * 16, 16), 16), :] = picked[:, b * BLK : (b + 1) * BLK]

    pl.semaphore_wait(barrier, 14)

    slot = 0
    s_copy = send(s_send, s_core, slot, partner)
    slot += 1
    w_copy = send(w_send, w_all.at[x, y, z, core], slot, partner)
    slot += 1

    g_copies = []
    for d in (1, 2, 3, 0):
        c = lax.rem(y + d, 4)
        cols = pl.ds(pl.multiple_of(c * BLK, BLK), BLK)
        g_send[d] = dot(oth_b[:, cols], oth_s[...], ((0,), (0,)))
        g_copies.append(send(g_send.at[d], g_core.at[d], slot, partner))
        slot += 1
        g_mine[d] = dot(mine_b[:, cols], mine_s[...], ((0,), (0,)))

    s_copy.wait_recv()
    for b in range(7):
        s_all[x, b, pl.ds(pl.multiple_of((1 - core) * 16, 16), 16), :] = s_core[b]
    s_copies = []
    for d in (1, 2, 3):
        s_copies.append(send(s_all.at[x], s_all.at[x], slot, x_peer[d]))
        slot += 1

    gy_copies = []
    for index, d in enumerate((1, 2, 3, 0)):
        g_copies[index].wait_recv()
        total = g_mine[d] + g_core[d]
        if d == 0:
            g_y[y] = total
        else:
            g_mine[d] = total
            gy_copies.append(send(g_mine.at[d], g_y.at[y], slot, y_peer[d]))
            slot += 1

    w_copy.wait_recv()
    w_copies = []
    for d in range(1, 8):
        w_copies.append(send(w_all.at[x, y, z], w_all.at[x, y, z], slot, z_peer[d]))
        slot += 1

    for copy in s_copies:
        copy.wait_recv()
    cy_copies = []
    for d in (1, 2, 3, 0):
        block = x * 4 + lax.rem(y + d, 4)
        left = lookup(block, [i for i, _ in PAIRS])
        right = lookup(block, [j for _, j in PAIRS])
        lhs = s_all[:, left].reshape(128, BLK)
        rhs = s_all[:, right].reshape(128, BLK)
        value = dot(lhs, rhs, ((0,), (0,)))
        if d == 0:
            c_y[y] = value
        else:
            c_part[d] = value
            cy_copies.append(send(c_part.at[d], c_y.at[y], slot, y_peer[d]))
            slot += 1

    for copy in w_copies:
        copy.wait_recv()
    w_copies = []
    for d in (1, 2, 3):
        w_copies.append(send(w_all.at[x, y], w_all.at[x, y], slot, y_peer[d]))
        slot += 1

    for copy in cy_copies:
        copy.wait_recv()
    c_ysum[...] = (c_y[0] + c_y[1]) + (c_y[2] + c_y[3])
    cz_copies = []
    for d in range(1, 8):
        rows = pl.ds(pl.multiple_of(lax.rem(z + d, 4) * 32, 32), 32)
        cz_copies.append(send(c_ysum.at[rows], c_z.at[z], slot, z_peer[d]))
        slot += 1
    c_z[z] = c_ysum[pl.ds(pl.multiple_of(own * 32, 32), 32), :]

    for copy in gy_copies:
        copy.wait_recv()
    g_ysum[...] = (g_y[0] + g_y[1]) + (g_y[2] + g_y[3])
    gx_copies = []
    for d in (1, 2, 3):
        rows = pl.ds(pl.multiple_of(lax.rem(x + d, 4) * 32, 32), 32)
        gx_copies.append(send(g_ysum.at[rows], g_x.at[x], slot, x_peer[d]))
        slot += 1
    g_x[x] = g_ysum[pl.ds(pl.multiple_of(x * 32, 32), 32), :]

    for copy in w_copies:
        copy.wait_recv()
    w_copies = []
    for d in (1, 2, 3):
        w_copies.append(send(w_all.at[x], w_all.at[x], slot, x_peer[d]))
        slot += 1

    my_block = x * 4 + y
    for copy in cz_copies:
        copy.wait_recv()
    total = c_z[0]
    for k in range(1, 8):
        total = total + c_z[k]
    c_rows = pl.ds(pl.multiple_of(own * 32, 32), 32)
    c_blocks[my_block, c_rows, :] = total
    cag_copies = []
    for d in (1, 7, 6):
        view = c_blocks.at[my_block, c_rows]
        cag_copies.append(send(view, view, slot, z_peer[d]))
        slot += 1

    for copy in gx_copies:
        copy.wait_recv()
    g_xsum[...] = (g_x[0] + g_x[1]) + (g_x[2] + g_x[3])
    gz_copies = []
    for d in range(1, 8):
        rows = pl.ds(pl.multiple_of(lax.rem(z + d, 4) * 8, 8), 8)
        gz_copies.append(send(g_xsum.at[rows], g_z.at[z], slot, z_peer[d]))
        slot += 1
    g_z[z] = g_xsum[pl.ds(pl.multiple_of(own * 8, 8), 8), :]

    for copy in cag_copies:
        copy.wait_recv()
    cag_copies = []
    for d in (1, 2, 3):
        view = c_blocks.at[my_block]
        cag_copies.append(send(view, view, slot, y_peer[d]))
        slot += 1

    for copy in gz_copies:
        copy.wait_recv()
    total = g_z[0]
    for k in range(1, 8):
        total = total + g_z[k]
    base = y * 128 + x * 32
    g_rows = pl.ds(pl.multiple_of(base + own * 8, 8), 8)
    g_full[g_rows, :] = total
    gag_copies = []
    for d in (1, 7, 6):
        gag_copies.append(send(g_full.at[g_rows], g_full.at[g_rows], slot, z_peer[d]))
        slot += 1

    for copy in cag_copies:
        copy.wait_recv()
    cag_copies = []
    for d in (1, 2, 3):
        view = c_blocks.at[pl.ds(x * 4, 4)]
        cag_copies.append(send(view, view, slot, x_peer[d]))
        slot += 1

    for copy in gag_copies:
        copy.wait_recv()
    gag_copies = []
    g_rows = pl.ds(pl.multiple_of(base, 32), 32)
    for d in (1, 2, 3):
        gag_copies.append(send(g_full.at[g_rows], g_full.at[g_rows], slot, x_peer[d]))
        slot += 1
    for copy in gag_copies:
        copy.wait_recv()
    gag_copies = []
    g_rows = pl.ds(pl.multiple_of(y * 128, 128), 128)
    for d in (1, 2, 3):
        gag_copies.append(send(g_full.at[g_rows], g_full.at[g_rows], slot, y_peer[d]))
        slot += 1

    for copy in w_copies:
        copy.wait_recv()

    @pl.when(core == 0)
    def _():
        def place(step, carry):
            wx, wy = step // 4, lax.rem(step, 4)
            for zh in range(2):
                for cc in range(2):
                    row = pl.multiple_of(((zh * 4 + wx) * 4 + wy) * 16 + cc * 8, 8)
                    for o in range(4):
                        new_q[pl.ds(row, 8), o * 96 : (o + 1) * 96] = w_all[
                            wx, wy, zh * 4 + o, cc, :, 0:96
                        ]
            return carry

        lax.fori_loop(0, 16, place, 0)

    @pl.when(core == 1)
    def _():
        def place(step, carry):
            zh, wx = step // 4, lax.rem(step, 4)
            row = pl.multiple_of(step * 48, 8)
            for o in range(4):
                parts = [
                    w_all[wx, wy, zh * 4 + o, cc, 0:6, :] for wy in range(4) for cc in range(2)
                ]
                new_o[pl.ds(row, 48), o * BLK : (o + 1) * BLK] = jnp.concatenate(parts, axis=0)
            return carry

        lax.fori_loop(0, 8, place, 0)

    fetch(start_aq, st_b, 4).wait()
    fetch(start_gq, st_s, 5).wait()
    for copy in cag_copies:
        copy.wait_recv()

    def factor(n, offset, st_ref, e_ref, p_ref):
        count = n // BLK
        where = {pair: position for position, pair in enumerate(PAIRS)}
        squares = jnp.zeros((1, 1), F32)
        for i in range(count):
            for j in range(i, count):
                block = c_blocks[where[(i + offset, j + offset)]] * (1.0 / SAMPLES)
                for a, b, value in ((i, j, block), (j, i, block.T)) if i != j else ((i, j, block),):
                    at = (slice(a * BLK, (a + 1) * BLK), slice(b * BLK, (b + 1) * BLK))
                    mixed = DECAY * st_ref[at] + (1.0 - DECAY) * value
                    if a == b:
                        mixed = mixed + jnp.where(eye_mask(BLK), DAMPING, 0.0)
                    e_ref[at] = mixed
                    row = jnp.sum(mixed * mixed, axis=0, keepdims=True)
                    squares = squares + jnp.sum(row, axis=1, keepdims=True)
        scale = 1.0 / jnp.sqrt(squares)
        for i in range(count):
            at = slice(i * BLK, (i + 1) * BLK)
            one = jnp.where(row_eye(i, n), 1.0, 0.0)
            rest = one - scale * e_ref[at, :]
            e_ref[at, :] = rest
            p_ref[at, :] = scale * (one + rest)

    factor(BIG, 0, st_b, e_b, p_b)
    factor(SMALL, 4, st_s, e_s, p_s)

    def iterate(step, carry):
        newton_step(BIG, e_b, p_b, eb_b, pb_b)
        newton_step(SMALL, e_s, p_s, eb_s, pb_s)
        return carry

    lax.fori_loop(0, 3, iterate, 0)

    for copy in gag_copies:
        copy.wait_recv()
    grad = high_low(g_full[...] * (1.0 / TOKENS))
    for i in range(4):
        at = slice(i * BLK, (i + 1) * BLK)
        m_ref[at, :] = dot3(high_low(p_b[at, :]), grad)

    @pl.when(core == 0)
    def _():
        right = high_low(p_s[...])
        for i in range(4):
            at = slice(i * BLK, (i + 1) * BLK)
            new_q[at, :] = new_q[at, :] - LEARNING_RATE * dot3(high_low(m_ref[at, :]), right)
        copy = remote(new_q, new_q, slot, partner)
        copy.start()
        copy.wait_send()
        remote(new_o, new_o, slot, partner).wait_recv()

    @pl.when(core == 1)
    def _():
        right = high_low(m_ref[...])
        for i in range(3):
            at = slice(i * BLK, (i + 1) * BLK)
            new_o[at, :] = new_o[at, :] - LEARNING_RATE * dot3(
                high_low(p_s[at, :]), right, ((1,), (1,))
            )
        copy = remote(new_o, new_o, slot, partner)
        copy.start()
        copy.wait_send()
        remote(new_q, new_q, slot, partner).wait_recv()

    for copy in pending:
        copy.wait_send()


COPIES = 80


def per_device(*args):
    hbm = pl.BlockSpec(memory_space=pl.ANY)
    vmem = pl.BlockSpec(memory_space=pltpu.VMEM)
    smem = pl.BlockSpec(memory_space=pltpu.SMEM)

    def v(shape, dtype=F32):
        return pltpu.VMEM(shape, dtype)

    return pl.pallas_call(
        kernel,
        out_shape=(
            jax.ShapeDtypeStruct((BIG, SMALL), F32),
            jax.ShapeDtypeStruct((SMALL, BIG), F32),
        ),
        in_specs=[hbm] * 4 + [smem] + [hbm] * 4 + [vmem] * 2,
        out_specs=(vmem, vmem),
        scratch_shapes=[
            v((1024, BIG), BF16), v((1024, SMALL), BF16), v((1024, BIG), BF16), v((1024, SMALL), BF16),
            v((BIG, BIG)), v((SMALL, SMALL)),
            v((4, BLK, SMALL)), v((4, BLK, SMALL)), v((4, BLK, SMALL)),
            v((4, BLK, SMALL)), v((BLK, SMALL)), v((4, 32, SMALL)), v((32, SMALL)), v((8, 8, SMALL)),
            v((BIG, SMALL)),
            v((7, 16, BLK), BF16), v((7, 16, BLK), BF16), v((4, 7, 32, BLK), BF16),
            v((4, BLK, BLK)), v((4, BLK, BLK)), v((BLK, BLK)), v((8, 32, BLK)), v((16, BLK, BLK)),
            v((8, BLK)), v((4, 4, 8, 2, 8, BLK)),
            v((BIG, BIG)), v((BIG, BIG)), v((BIG, BIG), BF16), v((BIG, BIG), BF16),
            v((SMALL, SMALL)), v((SMALL, SMALL)), v((SMALL, SMALL), BF16), v((SMALL, SMALL), BF16),
            v((BIG, SMALL)),
            pltpu.SemaphoreType.DMA((6,)),
            pltpu.SemaphoreType.DMA((COPIES,)),
            pltpu.SemaphoreType.DMA((COPIES,)),
        ],
        compiler_params=pltpu.CompilerParams(
            collective_id=0, has_side_effects=True, vmem_limit_bytes=64000000
        ),
    )(*args)


def solution(mesh):
    return jax.shard_map(
        per_device,
        mesh=mesh,
        in_specs=(P(("dp", "own"), None),) * 4
        + (P(("dp", "own")),)
        + (P(),) * 4
        + (P("dp", "own"),) * 2,
        out_specs=(P(), P()),
        check_vma=False,
    )
```

```python
import functools

import jax
import jax.numpy as jnp
from jax import lax
from jax.experimental import pallas as pl
from jax.experimental.pallas import tpu as pltpu
from jax.sharding import PartitionSpec as P

MESH = pl.DeviceIdType.MESH
F32 = jnp.float32
BF16 = jnp.bfloat16
DECAY = 0.5
DAMPING = 0.5
LEARNING_RATE = 10.0
TOKENS = 262144
SAMPLES = 4096
BIG = 512
SMALL = 384
BLK = 128
PAIRS = [(i, j) for i in range(4) for j in range(i, 4)] + [
    (i, j) for i in range(4, 7) for j in range(i, 7)
]


def lookup(index, table):
    value = jnp.int32(table[0])
    for position in range(1, len(table)):
        value = jnp.where(index == position, jnp.int32(table[position]), value)
    return value


def dot(a, b, dims=((1,), (0,))):
    return lax.dot_general(a, b, (dims, ((), ())), preferred_element_type=F32)


def high_low(value):
    high = value.astype(BF16)
    return high, (value - high.astype(F32)).astype(BF16)


def dot3(a, b, dims=((1,), (0,))):
    return dot(a[0], b[0], dims) + dot(a[0], b[1], dims) + dot(a[1], b[0], dims)


def eye_mask(n):
    return lax.broadcasted_iota(jnp.int32, (n, n), 0) == lax.broadcasted_iota(
        jnp.int32, (n, n), 1
    )


def diagonal(ref, n):
    mask = eye_mask(BLK)
    cols, rows = [], []
    for i in range(n // BLK):
        at = slice(i * BLK, (i + 1) * BLK)
        block = jnp.where(mask, ref[at, at], 0.0)
        cols.append(jnp.sum(block, axis=1, keepdims=True))
        rows.append(jnp.sum(block, axis=0, keepdims=True))
    return cols, jnp.concatenate(rows, axis=1)


def row_eye(i, n):
    return lax.broadcasted_iota(jnp.int32, (BLK, n), 0) + i * BLK == lax.broadcasted_iota(
        jnp.int32, (BLK, n), 1
    )


def newton_step(n, e_ref, p_ref, eb_ref, pb_ref):
    blocks = range(n // BLK)
    e_col, e_row = diagonal(e_ref, n)
    for i in blocks:
        at = slice(i * BLK, (i + 1) * BLK)
        eb_ref[at, :] = jnp.where(row_eye(i, n), 0.0, e_ref[at, :]).astype(BF16)
        pb_ref[at, :] = jnp.where(row_eye(i, n), 0.0, p_ref[at, :]).astype(BF16)
    for i in blocks:
        at = slice(i * BLK, (i + 1) * BLK)
        square = dot(eb_ref[at, :], eb_ref[...])
        rest = e_ref[at, :]
        weight = jnp.where(row_eye(i, n), e_col[i], e_col[i] + e_row)
        e_ref[at, :] = square + weight * rest
    f_col, f_row = diagonal(e_ref, n)
    p_col, _ = diagonal(p_ref, n)
    for i in blocks:
        at = slice(i * BLK, (i + 1) * BLK)
        eb_ref[at, :] = jnp.where(row_eye(i, n), 0.0, e_ref[at, :]).astype(BF16)
    for i in blocks:
        at = slice(i * BLK, (i + 1) * BLK)
        product = dot(pb_ref[at, :], eb_ref[...])
        p_rows = p_ref[at, :]
        off = jnp.where(row_eye(i, n), 0.0, e_ref[at, :])
        p_ref[at, :] = p_rows + product + p_col[i] * off + p_rows * f_row


def kernel(
    acts_q, grads_q, acts_o, grads_o, rows_ref,
    start_aq, start_gq, start_ao, start_go, wq_ref, wo_ref,
    new_q, new_o,
    mine_b, mine_s, oth_b, oth_s, st_b, st_s,
    g_send, g_mine, g_core, g_part, g_relay, g_got, g_sum, g_x, g_xsum, g_z, g_full,
    s_send, s_core, s_all,
    c_part, c_relay, c_got, c_ysum, c_z, c_blocks,
    w_send, w_all,
    e_b, p_b, eb_b, pb_b, e_s, p_s, eb_s, pb_s, m_ref,
    in_sem, send_sem, recv_sem,
):
    dp, own = lax.axis_index("dp"), lax.axis_index("own")
    core = lax.rem(dp, 2)
    y = lax.rem(dp // 2, 4)
    x = lax.rem(dp // 8, 4)
    z = (dp // 32) * 4 + own

    def device(cx, cy, cz, cc):
        return ((cz // 4) * 32 + cx * 8 + cy * 2 + cc, lax.rem(cz, 4))

    partner = device(x, y, z, 1 - core)
    x_peer = [device(lax.rem(x + d, 4), y, z, core) for d in range(4)]
    y_peer = [device(x, lax.rem(y + d, 4), z, core) for d in range(4)]
    z_peer = [device(x, y, lax.rem(z + d, 8), core) for d in range(8)]

    def fetch(src, dst, sem):
        return pltpu.make_async_copy(src, dst, in_sem.at[sem])

    @pl.when(core == 0)
    def _():
        fetch(acts_q, mine_b, 0).start()
        fetch(grads_q, mine_s, 1).start()
        fetch(grads_o, oth_b, 2).start()
        fetch(acts_o, oth_s, 3).start()
        fetch(start_aq, st_b, 4).start()
        fetch(start_gq, st_s, 5).start()

    @pl.when(core == 1)
    def _():
        fetch(grads_o, mine_b, 0).start()
        fetch(acts_o, mine_s, 1).start()
        fetch(acts_q, oth_b, 2).start()
        fetch(grads_q, oth_s, 3).start()
        fetch(start_go, st_b, 4).start()
        fetch(start_ao, st_s, 5).start()

    barrier = pltpu.get_barrier_semaphore()
    for peer in [partner] + x_peer[1:] + y_peer[1:] + z_peer[1:]:
        pl.semaphore_signal(barrier, inc=1, device_id=peer, device_id_type=MESH)

    def remote(src, dst, slot, peer):
        return pltpu.make_async_remote_copy(
            src_ref=src, dst_ref=dst, send_sem=send_sem.at[slot],
            recv_sem=recv_sem.at[slot], device_id=peer, device_id_type=MESH,
        )

    pending = []

    def send(src, dst, peer):
        copy = remote(src, dst, len(pending), peer)
        copy.start()
        pending.append(copy)
        return copy

    def land(copies):
        for copy in copies:
            copy.wait_recv()

    def spread(view, peers):
        return [send(view, view, peer) for peer in peers]

    class Scatter:
        def __init__(self, buf, relay, got, me, peer):
            self.buf, self.relay, self.got, self.me, self.peer = buf, relay, got, me, peer
            far, self.after, self.before = (lax.rem(me + d, 4) for d in (2, 1, 3))
            self.first = [
                send(buf.at[far, 0], relay.at[0], peer[1]),
                send(buf.at[far, 1], relay.at[1], peer[3]),
            ]
            self.rest = [
                send(buf.at[self.after, 1], got.at[0, 1], peer[1]),
                send(buf.at[self.before, 0], got.at[1, 0], peer[3]),
            ]

        def forward(self):
            for part, (chunk, peer) in enumerate(((self.after, self.peer[1]), (self.before, self.peer[3]))):
                self.first[part].wait_recv()
                self.buf[chunk, part] = self.buf[chunk, part] + self.relay[part]
                self.rest.append(send(self.buf.at[chunk, part], self.got.at[part, part], peer))

        def sums(self):
            land(self.rest)
            return [(self.buf[self.me, p] + self.got[0, p]) + self.got[1, p] for p in range(2)]

    class Gather:
        def __init__(self, view, me, peer):
            self.view, self.peer = view, peer
            self.after, self.before = lax.rem(me + 1, 4), lax.rem(me + 3, 4)
            mine = [view(me, 0), view(me, 1)]
            self.first = [send(mine[0], mine[0], peer[1]), send(mine[1], mine[1], peer[3])]
            self.rest = [send(mine[1], mine[1], peer[1]), send(mine[0], mine[0], peer[3])]

        def forward(self):
            for part, (chunk, peer) in enumerate(((self.before, self.peer[1]), (self.after, self.peer[3]))):
                self.first[part].wait_recv()
                view = self.view(chunk, part)
                self.rest.append(send(view, view, peer))

        def finish(self):
            land(self.rest)

    w_send[...] = jnp.zeros_like(w_send)

    @pl.when(core == 0)
    def _():
        w_all[x, y, z, 0] = jnp.zeros((8, BLK), F32)
        w_all[x, y, z, 0, :, 0:96] = wq_ref[...]
        w_send[0:6, :] = wo_ref[...]

    @pl.when(core == 1)
    def _():
        w_all[x, y, z, 1] = jnp.zeros((8, BLK), F32)
        w_all[x, y, z, 1, 0:6, :] = wo_ref[...]
        w_send[:, 0:96] = wq_ref[...]

    fetch(acts_q, oth_b, 2).wait()
    fetch(grads_q, oth_s, 3).wait()
    fetch(acts_q, mine_b, 0).wait()
    fetch(grads_q, mine_s, 1).wait()

    target = jnp.zeros((16, 1024), jnp.int32)
    row = lax.broadcasted_iota(jnp.int32, (16, 1024), 0)
    for k in range(16):
        target = jnp.where(row == k, rows_ref[k], target)
    pick = lax.broadcasted_iota(jnp.int32, (16, 1024), 1) == target
    one_hot = jnp.where(pick, 1.0, 0.0).astype(BF16)

    def sampled(big, small):
        return jnp.concatenate([dot(one_hot, big[...]), dot(one_hot, small[...])], axis=1).astype(BF16)

    picked = sampled(oth_b, oth_s)
    for b in range(7):
        s_send[b] = picked[:, b * BLK : (b + 1) * BLK]
    picked = sampled(mine_b, mine_s)
    for b in range(7):
        s_all[x, b, pl.ds(pl.multiple_of(core * 16, 16), 16), :] = picked[:, b * BLK : (b + 1) * BLK]

    pl.semaphore_wait(barrier, 14)

    s_copy = send(s_send, s_core, partner)
    w_copy = send(w_send, w_all.at[x, y, z, core], partner)

    g_copies = []
    for d in (2, 1, 3, 0):
        c = lax.rem(y + d, 4)
        cols = pl.ds(pl.multiple_of(c * BLK, BLK), BLK)
        g_send[d] = dot(oth_b[:, cols], oth_s[...], ((0,), (0,)))
        g_copies.append(send(g_send.at[d], g_core.at[d], partner))
        if d == 2:
            s_copy.wait_recv()
            for b in range(7):
                s_all[x, b, pl.ds(pl.multiple_of((1 - core) * 16, 16), 16), :] = s_core[b]
            s_gather = Gather(lambda i, p: s_all.at[i, pl.ds(4 * p, 4 - p)], x, x_peer)
        g_mine[d] = dot(mine_b[:, cols], mine_s[...], ((0,), (0,)))

    w_copy.wait_recv()
    w_copies = spread(w_all.at[x, y, z], z_peer[1:])
    s_gather.forward()

    for index, d in enumerate((2, 1, 3, 0)):
        c = lax.rem(y + d, 4)
        g_copies[index].wait_recv()
        total = g_mine[d] + g_core[d]
        for b in range(4):
            g_part[0, c, b // 2, b % 2] = total[b * 32 : b * 32 + 16]
            g_part[1, b, c // 2, lax.rem(c, 2)] = total[b * 32 + 16 : b * 32 + 32]
    g_scatter = [
        Scatter(g_part.at[0], g_relay.at[0], g_got.at[0], y, y_peer),
        Scatter(g_part.at[1], g_relay.at[1], g_got.at[1], x, x_peer),
    ]

    s_gather.finish()
    for d in (2, 1, 3, 0):
        c = lax.rem(y + d, 4)
        block = x * 4 + c
        left = lookup(block, [i for i, _ in PAIRS])
        right = lookup(block, [j for _, j in PAIRS])
        lhs = s_all[:, left].reshape(128, BLK)
        rhs = s_all[:, right].reshape(128, BLK)
        value = dot(lhs, rhs, ((0,), (0,)))
        c_part[c, 0] = value[0:64]
        c_part[c, 1] = value[64:128]
    c_scatter = Scatter(c_part, c_relay, c_got, y, y_peer)
    g_scatter[0].forward()
    g_scatter[1].forward()
    c_scatter.forward()

    for p, value in enumerate(c_scatter.sums()):
        c_ysum[p * 64 : (p + 1) * 64, :] = value
    cz_copies = []
    for d in range(1, 8):
        rows = pl.ds(pl.multiple_of(lax.rem(z + d, 4) * 32, 32), 32)
        cz_copies.append(send(c_ysum.at[rows], c_z.at[z], z_peer[d]))
    c_z[z] = c_ysum[pl.ds(pl.multiple_of(own * 32, 32), 32), :]

    for h in range(2):
        for p, value in enumerate(g_scatter[h].sums()):
            g_sum[h, p] = value
    gx_copies = []
    for d in (1, 2, 3):
        to = lax.rem(x + d, 4)
        gx_copies.append(send(g_sum.at[0, to // 2, lax.rem(to, 2)], g_x.at[0, x], x_peer[d]))
        to = lax.rem(y + d, 4)
        gx_copies.append(send(g_sum.at[1, to // 2, lax.rem(to, 2)], g_x.at[1, y], y_peer[d]))
    g_x[0, x] = g_sum[0, x // 2, lax.rem(x, 2)]
    g_x[1, y] = g_sum[1, y // 2, lax.rem(y, 2)]

    land(gx_copies)
    for h in range(2):
        g_xsum[h * 16 : (h + 1) * 16, :] = (g_x[h, 0] + g_x[h, 1]) + (g_x[h, 2] + g_x[h, 3])
    gz_copies = []
    for d in range(1, 8):
        rows = pl.ds(pl.multiple_of(lax.rem(z + d, 4) * 8, 8), 8)
        gz_copies.append(send(g_xsum.at[rows], g_z.at[z], z_peer[d]))
    g_z[z] = g_xsum[pl.ds(pl.multiple_of(own * 8, 8), 8), :]

    land(w_copies)
    w_copies = spread(w_all.at[x, y, pl.ds(0, 4)], y_peer[1:])
    w_copies += spread(w_all.at[x, y, pl.ds(4, 4)], x_peer[1:])

    land(cz_copies)
    total = c_z[0]
    for k in range(1, 8):
        total = total + c_z[k]
    c_view = (x, y, own // 2, pl.ds(pl.multiple_of(lax.rem(own, 2) * 32, 32), 32))
    c_blocks[c_view] = total
    cag_copies = spread(c_blocks.at[c_view], [z_peer[d] for d in (1, 7, 6)])

    land(w_copies)
    w_gather = [
        Gather(lambda i, p: w_all.at[i, pl.ds(2 * p, 2), pl.ds(0, 4)], x, x_peer),
        Gather(lambda i, p: w_all.at[pl.ds(2 * p, 2), i, pl.ds(4, 4)], y, y_peer),
    ]

    land(cag_copies)
    cag_copies = spread(c_blocks.at[x, y, 0], y_peer[1:]) + spread(c_blocks.at[x, y, 1], x_peer[1:])

    land(gz_copies)
    total = g_z[0]
    for k in range(1, 8):
        total = total + g_z[k]
    g_view = (y, x, pl.ds(pl.multiple_of(own * 8, 8), 8))
    g_full[g_view] = total
    gag_copies = spread(g_full.at[g_view], [z_peer[d] for d in (1, 7, 6)])

    w_gather[0].forward()
    w_gather[1].forward()

    land(cag_copies)
    c_gather = [
        Gather(lambda i, p: c_blocks.at[i, pl.ds(2 * p, 2), 0], x, x_peer),
        Gather(lambda i, p: c_blocks.at[pl.ds(2 * p, 2), i, 1], y, y_peer),
    ]

    land(gag_copies)
    gag_copies = spread(g_full.at[y, x, pl.ds(0, 16)], x_peer[1:])
    gag_copies += spread(g_full.at[y, x, pl.ds(16, 16)], y_peer[1:])
    c_gather[0].forward()
    c_gather[1].forward()
    land(gag_copies)
    g_gather = [
        Gather(lambda i, p: g_full.at[i, pl.ds(2 * p, 2), pl.ds(0, 16)], y, y_peer),
        Gather(lambda i, p: g_full.at[pl.ds(2 * p, 2), i, pl.ds(16, 16)], x, x_peer),
    ]

    w_gather[0].finish()
    w_gather[1].finish()

    @pl.when(core == 0)
    def _():
        def place(step, carry):
            wx, wy = step // 4, lax.rem(step, 4)
            for zh in range(2):
                for cc in range(2):
                    row = pl.multiple_of(((zh * 4 + wx) * 4 + wy) * 16 + cc * 8, 8)
                    for o in range(4):
                        new_q[pl.ds(row, 8), o * 96 : (o + 1) * 96] = w_all[
                            wx, wy, zh * 4 + o, cc, :, 0:96
                        ]
            return carry

        lax.fori_loop(0, 16, place, 0)

    @pl.when(core == 1)
    def _():
        def place(step, carry):
            zh, wx = step // 4, lax.rem(step, 4)
            row = pl.multiple_of(step * 48, 8)
            for o in range(4):
                parts = [
                    w_all[wx, wy, zh * 4 + o, cc, 0:6, :] for wy in range(4) for cc in range(2)
                ]
                new_o[pl.ds(row, 48), o * BLK : (o + 1) * BLK] = jnp.concatenate(parts, axis=0)
            return carry

        lax.fori_loop(0, 8, place, 0)

    fetch(start_aq, st_b, 4).wait()
    fetch(start_gq, st_s, 5).wait()
    c_gather[0].finish()
    c_gather[1].finish()

    def factor(n, offset, st_ref, e_ref, p_ref):
        count = n // BLK
        where = {pair: position for position, pair in enumerate(PAIRS)}
        squares = jnp.zeros((1, 1), F32)
        for i in range(count):
            for j in range(i, count):
                position = where[(i + offset, j + offset)]
                block = c_blocks[position // 4, position % 4].reshape(BLK, BLK) * (1.0 / SAMPLES)
                for a, b, value in ((i, j, block), (j, i, block.T)) if i != j else ((i, j, block),):
                    at = (slice(a * BLK, (a + 1) * BLK), slice(b * BLK, (b + 1) * BLK))
                    mixed = DECAY * st_ref[at] + (1.0 - DECAY) * value
                    if a == b:
                        mixed = mixed + jnp.where(eye_mask(BLK), DAMPING, 0.0)
                    e_ref[at] = mixed
                    row = jnp.sum(mixed * mixed, axis=0, keepdims=True)
                    squares = squares + jnp.sum(row, axis=1, keepdims=True)
        scale = 1.0 / jnp.sqrt(squares)
        for i in range(count):
            at = slice(i * BLK, (i + 1) * BLK)
            one = jnp.where(row_eye(i, n), 1.0, 0.0)
            rest = one - scale * e_ref[at, :]
            e_ref[at, :] = rest
            p_ref[at, :] = scale * (one + rest)

    factor(BIG, 0, st_b, e_b, p_b)
    g_gather[0].forward()
    g_gather[1].forward()
    factor(SMALL, 4, st_s, e_s, p_s)

    def iterate(step, carry):
        newton_step(BIG, e_b, p_b, eb_b, pb_b)
        newton_step(SMALL, e_s, p_s, eb_s, pb_s)
        return carry

    lax.fori_loop(0, 3, iterate, 0)

    g_gather[0].finish()
    g_gather[1].finish()
    grad = high_low(g_full[...].reshape(BIG, SMALL) * (1.0 / TOKENS))
    for i in range(4):
        at = slice(i * BLK, (i + 1) * BLK)
        m_ref[at, :] = dot3(high_low(p_b[at, :]), grad)
    slot = len(pending)

    def rows_of(ref, i):
        view = ref.at[pl.ds(i * BLK, BLK)]
        return remote(view, view, slot + i, partner)

    @pl.when(core == 0)
    def _():
        right = high_low(p_s[...])
        for i in range(4):
            at = slice(i * BLK, (i + 1) * BLK)
            new_q[at, :] = new_q[at, :] - LEARNING_RATE * dot3(high_low(m_ref[at, :]), right)
            rows_of(new_q, i).start()
        for i in range(4):
            rows_of(new_q, i).wait_send()
        for i in range(3):
            rows_of(new_o, i).wait_recv()

    @pl.when(core == 1)
    def _():
        right = high_low(m_ref[...])
        for i in range(3):
            at = slice(i * BLK, (i + 1) * BLK)
            new_o[at, :] = new_o[at, :] - LEARNING_RATE * dot3(
                high_low(p_s[at, :]), right, ((1,), (1,))
            )
            rows_of(new_o, i).start()
        for i in range(3):
            rows_of(new_o, i).wait_send()
        for i in range(4):
            rows_of(new_q, i).wait_recv()

    for copy in pending:
        copy.wait_send()


COPIES = 128


def per_device(*args):
    hbm = pl.BlockSpec(memory_space=pl.ANY)
    vmem = pl.BlockSpec(memory_space=pltpu.VMEM)
    smem = pl.BlockSpec(memory_space=pltpu.SMEM)

    def v(shape, dtype=F32):
        return pltpu.VMEM(shape, dtype)

    return pl.pallas_call(
        kernel,
        out_shape=(
            jax.ShapeDtypeStruct((BIG, SMALL), F32),
            jax.ShapeDtypeStruct((SMALL, BIG), F32),
        ),
        in_specs=[hbm] * 4 + [smem] + [hbm] * 4 + [vmem] * 2,
        out_specs=(vmem, vmem),
        scratch_shapes=[
            v((1024, BIG), BF16), v((1024, SMALL), BF16), v((1024, BIG), BF16), v((1024, SMALL), BF16),
            v((BIG, BIG)), v((SMALL, SMALL)),
            v((4, BLK, SMALL)), v((4, BLK, SMALL)), v((4, BLK, SMALL)),
            v((2, 4, 2, 2, 16, SMALL)), v((2, 2, 2, 16, SMALL)), v((2, 2, 2, 2, 16, SMALL)),
            v((2, 2, 2, 16, SMALL)), v((2, 4, 16, SMALL)), v((32, SMALL)), v((8, 8, SMALL)),
            v((4, 4, 32, SMALL)),
            v((7, 16, BLK), BF16), v((7, 16, BLK), BF16), v((4, 7, 32, BLK), BF16),
            v((4, 2, 64, BLK)), v((2, 64, BLK)), v((2, 2, 64, BLK)),
            v((BLK, BLK)), v((8, 32, BLK)), v((4, 4, 2, 64, BLK)),
            v((8, BLK)), v((4, 4, 8, 2, 8, BLK)),
            v((BIG, BIG)), v((BIG, BIG)), v((BIG, BIG), BF16), v((BIG, BIG), BF16),
            v((SMALL, SMALL)), v((SMALL, SMALL)), v((SMALL, SMALL), BF16), v((SMALL, SMALL), BF16),
            v((BIG, SMALL)),
            pltpu.SemaphoreType.DMA((6,)),
            pltpu.SemaphoreType.DMA((COPIES,)),
            pltpu.SemaphoreType.DMA((COPIES,)),
        ],
        compiler_params=pltpu.CompilerParams(
            collective_id=0, has_side_effects=True, vmem_limit_bytes=64000000
        ),
    )(*args)


def solution(mesh):
    return jax.shard_map(
        per_device,
        mesh=mesh,
        in_specs=(P(("dp", "own"), None),) * 4
        + (P(("dp", "own")),)
        + (P(),) * 4
        + (P("dp", "own"),) * 2,
        out_specs=(P(), P()),
        check_vma=False,
    )
```

```python
import functools

import jax
import jax.numpy as jnp
from jax import lax
from jax.experimental import pallas as pl
from jax.experimental.pallas import tpu as pltpu
from jax.sharding import PartitionSpec as P

MESH = pl.DeviceIdType.MESH
F32 = jnp.float32
BF16 = jnp.bfloat16
DECAY = 0.5
DAMPING = 0.5
LEARNING_RATE = 10.0
TOKENS = 262144
SAMPLES = 4096
BIG = 512
SMALL = 384
BLK = 128
PAIRS = [(i, j) for i in range(4) for j in range(i, 4)] + [
    (i, j) for i in range(4, 7) for j in range(i, 7)
]


def lookup(index, table):
    value = jnp.int32(table[0])
    for position in range(1, len(table)):
        value = jnp.where(index == position, jnp.int32(table[position]), value)
    return value


def dot(a, b, dims=((1,), (0,))):
    return lax.dot_general(a, b, (dims, ((), ())), preferred_element_type=F32)


def high_low(value):
    high = value.astype(BF16)
    return high, (value - high.astype(F32)).astype(BF16)


def dot3(a, b, dims=((1,), (0,))):
    return dot(a[0], b[0], dims) + dot(a[0], b[1], dims) + dot(a[1], b[0], dims)


def eye_mask(n):
    return lax.broadcasted_iota(jnp.int32, (n, n), 0) == lax.broadcasted_iota(
        jnp.int32, (n, n), 1
    )


def diagonal(ref, n):
    mask = eye_mask(BLK)
    cols, rows = [], []
    for i in range(n // BLK):
        at = slice(i * BLK, (i + 1) * BLK)
        block = jnp.where(mask, ref[at, at], 0.0)
        cols.append(jnp.sum(block, axis=1, keepdims=True))
        rows.append(jnp.sum(block, axis=0, keepdims=True))
    return cols, jnp.concatenate(rows, axis=1)


def row_eye(i, n):
    return lax.broadcasted_iota(jnp.int32, (BLK, n), 0) + i * BLK == lax.broadcasted_iota(
        jnp.int32, (BLK, n), 1
    )


def newton_step(n, e_ref, p_ref, eb_ref, pb_ref):
    blocks = range(n // BLK)
    e_col, e_row = diagonal(e_ref, n)
    for i in blocks:
        at = slice(i * BLK, (i + 1) * BLK)
        eb_ref[at, :] = jnp.where(row_eye(i, n), 0.0, e_ref[at, :]).astype(BF16)
        pb_ref[at, :] = jnp.where(row_eye(i, n), 0.0, p_ref[at, :]).astype(BF16)
    for i in blocks:
        at = slice(i * BLK, (i + 1) * BLK)
        square = dot(eb_ref[at, :], eb_ref[...])
        rest = e_ref[at, :]
        weight = jnp.where(row_eye(i, n), e_col[i], e_col[i] + e_row)
        e_ref[at, :] = square + weight * rest
    f_col, f_row = diagonal(e_ref, n)
    p_col, _ = diagonal(p_ref, n)
    for i in blocks:
        at = slice(i * BLK, (i + 1) * BLK)
        eb_ref[at, :] = jnp.where(row_eye(i, n), 0.0, e_ref[at, :]).astype(BF16)
    for i in blocks:
        at = slice(i * BLK, (i + 1) * BLK)
        product = dot(pb_ref[at, :], eb_ref[...])
        p_rows = p_ref[at, :]
        off = jnp.where(row_eye(i, n), 0.0, e_ref[at, :])
        p_ref[at, :] = p_rows + product + p_col[i] * off + p_rows * f_row


def kernel(
    acts_q, grads_q, acts_o, grads_o, rows_ref,
    start_aq, start_gq, start_ao, start_go, wq_ref, wo_ref,
    new_q, new_o,
    mine_b, mine_s, oth_b, oth_s, st_b, st_s,
    g_send, g_mine, g_core, g_part, g_relay, g_got, g_sum, g_x, g_xsum, g_z, g_full,
    s_send, s_core, s_all,
    c_part, c_relay, c_got, c_ysum, c_z, c_blocks,
    w_send, w_all,
    e_b, p_b, eb_b, pb_b, e_s, p_s, eb_s, pb_s, m_ref,
    in_sem, send_sem, recv_sem,
):
    dp, own = lax.axis_index("dp"), lax.axis_index("own")
    core = lax.rem(dp, 2)
    y = lax.rem(dp // 2, 4)
    x = lax.rem(dp // 8, 4)
    z = (dp // 32) * 4 + own

    def device(cx, cy, cz, cc):
        return ((cz // 4) * 32 + cx * 8 + cy * 2 + cc, lax.rem(cz, 4))

    partner = device(x, y, z, 1 - core)
    x_peer = [device(lax.rem(x + d, 4), y, z, core) for d in range(4)]
    y_peer = [device(x, lax.rem(y + d, 4), z, core) for d in range(4)]
    z_peer = [device(x, y, lax.rem(z + d, 8), core) for d in range(8)]

    def fetch(src, dst, sem):
        return pltpu.make_async_copy(src, dst, in_sem.at[sem])

    @pl.when(core == 0)
    def _():
        fetch(acts_q, mine_b, 0).start()
        fetch(grads_q, mine_s, 1).start()
        fetch(grads_o, oth_b, 2).start()
        fetch(acts_o, oth_s, 3).start()
        fetch(start_aq, st_b, 4).start()
        fetch(start_gq, st_s, 5).start()

    @pl.when(core == 1)
    def _():
        fetch(grads_o, mine_b, 0).start()
        fetch(acts_o, mine_s, 1).start()
        fetch(acts_q, oth_b, 2).start()
        fetch(grads_q, oth_s, 3).start()
        fetch(start_go, st_b, 4).start()
        fetch(start_ao, st_s, 5).start()

    barrier = pltpu.get_barrier_semaphore()
    for peer in [partner] + x_peer[1:] + y_peer[1:] + z_peer[1:]:
        pl.semaphore_signal(barrier, inc=1, device_id=peer, device_id_type=MESH)

    def remote(src, dst, slot, peer):
        return pltpu.make_async_remote_copy(
            src_ref=src, dst_ref=dst, send_sem=send_sem.at[slot],
            recv_sem=recv_sem.at[slot], device_id=peer, device_id_type=MESH,
        )

    pending = []

    def send(src, dst, peer):
        copy = remote(src, dst, len(pending), peer)
        copy.start()
        pending.append(copy)
        return copy

    def land(copies):
        for copy in copies:
            copy.wait_recv()

    def spread(view, peers):
        return [send(view, view, peer) for peer in peers]

    class Scatter:
        def __init__(self, buf, relay, got, me, peer):
            self.buf, self.relay, self.got, self.me, self.peer = buf, relay, got, me, peer
            far, self.after, self.before = (lax.rem(me + d, 4) for d in (2, 1, 3))
            self.first = [
                send(buf.at[far, 0], relay.at[0], peer[1]),
                send(buf.at[far, 1], relay.at[1], peer[3]),
            ]
            self.rest = [
                send(buf.at[self.after, 1], got.at[0, 1], peer[1]),
                send(buf.at[self.before, 0], got.at[1, 0], peer[3]),
            ]

        def forward(self):
            for part, (chunk, peer) in enumerate(((self.after, self.peer[1]), (self.before, self.peer[3]))):
                self.first[part].wait_recv()
                self.buf[chunk, part] = self.buf[chunk, part] + self.relay[part]
                self.rest.append(send(self.buf.at[chunk, part], self.got.at[part, part], peer))

        def sums(self):
            land(self.rest)
            return [(self.buf[self.me, p] + self.got[0, p]) + self.got[1, p] for p in range(2)]

    class Gather:
        def __init__(self, view, me, peer):
            self.view, self.peer = view, peer
            self.after, self.before = lax.rem(me + 1, 4), lax.rem(me + 3, 4)
            mine = [view(me, 0), view(me, 1)]
            self.first = [send(mine[0], mine[0], peer[1]), send(mine[1], mine[1], peer[3])]
            self.rest = [send(mine[1], mine[1], peer[1]), send(mine[0], mine[0], peer[3])]

        def forward(self):
            for part, (chunk, peer) in enumerate(((self.before, self.peer[1]), (self.after, self.peer[3]))):
                self.first[part].wait_recv()
                view = self.view(chunk, part)
                self.rest.append(send(view, view, peer))

        def finish(self):
            land(self.rest)

    w_send[...] = jnp.zeros_like(w_send)

    @pl.when(core == 0)
    def _():
        w_all[x, y, z, 0] = jnp.zeros((8, BLK), F32)
        w_all[x, y, z, 0, :, 0:96] = wq_ref[...]
        w_send[0:6, :] = wo_ref[...]

    @pl.when(core == 1)
    def _():
        w_all[x, y, z, 1] = jnp.zeros((8, BLK), F32)
        w_all[x, y, z, 1, 0:6, :] = wo_ref[...]
        w_send[:, 0:96] = wq_ref[...]

    fetch(acts_q, oth_b, 2).wait()
    fetch(grads_q, oth_s, 3).wait()
    fetch(acts_q, mine_b, 0).wait()
    fetch(grads_q, mine_s, 1).wait()

    target = jnp.zeros((16, 1024), jnp.int32)
    row = lax.broadcasted_iota(jnp.int32, (16, 1024), 0)
    for k in range(16):
        target = jnp.where(row == k, rows_ref[k], target)
    pick = lax.broadcasted_iota(jnp.int32, (16, 1024), 1) == target
    one_hot = jnp.where(pick, 1.0, 0.0).astype(BF16)

    def sampled(big, small):
        return jnp.concatenate([dot(one_hot, big[...]), dot(one_hot, small[...])], axis=1).astype(BF16)

    picked = sampled(oth_b, oth_s)
    for b in range(7):
        s_send[b] = picked[:, b * BLK : (b + 1) * BLK]
    picked = sampled(mine_b, mine_s)
    for b in range(7):
        s_all[x, b, pl.ds(pl.multiple_of(core * 16, 16), 16), :] = picked[:, b * BLK : (b + 1) * BLK]

    pl.semaphore_wait(barrier, 14)

    s_copy = send(s_send, s_core, partner)
    w_copy = send(w_send, w_all.at[x, y, z, core], partner)

    g_copies = []
    for d in (2, 1, 3, 0):
        c = lax.rem(y + d, 4)
        cols = pl.ds(pl.multiple_of(c * BLK, BLK), BLK)
        g_send[d] = dot(oth_b[:, cols], oth_s[...], ((0,), (0,)))
        g_copies.append(send(g_send.at[d], g_core.at[d], partner))
        if d == 2:
            s_copy.wait_recv()
            for b in range(7):
                s_all[x, b, pl.ds(pl.multiple_of((1 - core) * 16, 16), 16), :] = s_core[b]
            s_gather = Gather(lambda i, p: s_all.at[i, pl.ds(4 * p, 4 - p)], x, x_peer)
        g_mine[d] = dot(mine_b[:, cols], mine_s[...], ((0,), (0,)))

    w_copy.wait_recv()
    w_copies = spread(w_all.at[x, y, z], z_peer[1:])
    s_gather.forward()

    for index, d in enumerate((2, 1, 3, 0)):
        c = lax.rem(y + d, 4)
        g_copies[index].wait_recv()
        total = g_mine[d] + g_core[d]
        for b in range(4):
            g_part[0, c, b // 2, b % 2] = total[b * 32 : b * 32 + 16]
            g_part[1, b, c // 2, lax.rem(c, 2)] = total[b * 32 + 16 : b * 32 + 32]
    g_scatter = [
        Scatter(g_part.at[0], g_relay.at[0], g_got.at[0], y, y_peer),
        Scatter(g_part.at[1], g_relay.at[1], g_got.at[1], x, x_peer),
    ]

    s_gather.finish()
    for d in (2, 1, 3, 0):
        c = lax.rem(y + d, 4)
        block = x * 4 + c
        left = lookup(block, [i for i, _ in PAIRS])
        right = lookup(block, [j for _, j in PAIRS])
        lhs = s_all[:, left].reshape(128, BLK)
        rhs = s_all[:, right].reshape(128, BLK)
        value = dot(lhs, rhs, ((0,), (0,)))
        c_part[c, 0] = value[0:64]
        c_part[c, 1] = value[64:128]
    c_scatter = Scatter(c_part, c_relay, c_got, y, y_peer)
    g_scatter[0].forward()
    g_scatter[1].forward()
    c_scatter.forward()

    for p, value in enumerate(c_scatter.sums()):
        c_ysum[p * 64 : (p + 1) * 64, :] = value
    cz_copies = []
    for d in range(1, 8):
        rows = pl.ds(pl.multiple_of(lax.rem(z + d, 4) * 32, 32), 32)
        cz_copies.append(send(c_ysum.at[rows], c_z.at[z], z_peer[d]))
    c_z[z] = c_ysum[pl.ds(pl.multiple_of(own * 32, 32), 32), :]

    for h in range(2):
        for p, value in enumerate(g_scatter[h].sums()):
            g_sum[h, p] = value
    gx_copies = []
    for d in (1, 2, 3):
        to = lax.rem(x + d, 4)
        gx_copies.append(send(g_sum.at[0, to // 2, lax.rem(to, 2)], g_x.at[0, x], x_peer[d]))
        to = lax.rem(y + d, 4)
        gx_copies.append(send(g_sum.at[1, to // 2, lax.rem(to, 2)], g_x.at[1, y], y_peer[d]))
    g_x[0, x] = g_sum[0, x // 2, lax.rem(x, 2)]
    g_x[1, y] = g_sum[1, y // 2, lax.rem(y, 2)]

    land(gx_copies)
    for h in range(2):
        g_xsum[h * 16 : (h + 1) * 16, :] = (g_x[h, 0] + g_x[h, 1]) + (g_x[h, 2] + g_x[h, 3])
    gz_copies = []
    for d in range(1, 8):
        rows = pl.ds(pl.multiple_of(lax.rem(z + d, 4) * 8, 8), 8)
        gz_copies.append(send(g_xsum.at[rows], g_z.at[z], z_peer[d]))
    g_z[z] = g_xsum[pl.ds(pl.multiple_of(own * 8, 8), 8), :]

    land(w_copies)
    w_copies = spread(w_all.at[x, y, pl.ds(0, 4)], y_peer[1:])
    w_copies += spread(w_all.at[x, y, pl.ds(4, 4)], x_peer[1:])

    land(cz_copies)
    total = c_z[0]
    for k in range(1, 8):
        total = total + c_z[k]
    c_view = (x, y, own // 2, pl.ds(pl.multiple_of(lax.rem(own, 2) * 32, 32), 32))
    c_blocks[c_view] = total
    cag_copies = spread(c_blocks.at[c_view], [z_peer[d] for d in (1, 7, 6)])

    land(cag_copies)
    cag_copies = spread(c_blocks.at[x, y, 0], y_peer[1:]) + spread(c_blocks.at[x, y, 1], x_peer[1:])

    land(gz_copies)
    total = g_z[0]
    for k in range(1, 8):
        total = total + g_z[k]
    g_view = (y, x, pl.ds(pl.multiple_of(own * 8, 8), 8))
    g_full[g_view] = total
    gag_copies = spread(g_full.at[g_view], [z_peer[d] for d in (1, 7, 6)])

    land(cag_copies)
    c_gather = [
        Gather(lambda i, p: c_blocks.at[i, pl.ds(2 * p, 2), 0], x, x_peer),
        Gather(lambda i, p: c_blocks.at[pl.ds(2 * p, 2), i, 1], y, y_peer),
    ]

    land(gag_copies)
    gag_copies = spread(g_full.at[y, x, pl.ds(0, 16)], x_peer[1:])
    gag_copies += spread(g_full.at[y, x, pl.ds(16, 16)], y_peer[1:])
    c_gather[0].forward()
    c_gather[1].forward()
    land(gag_copies)
    g_gather = [
        Gather(lambda i, p: g_full.at[i, pl.ds(2 * p, 2), pl.ds(0, 16)], y, y_peer),
        Gather(lambda i, p: g_full.at[pl.ds(2 * p, 2), i, pl.ds(16, 16)], x, x_peer),
    ]

    land(w_copies)
    w_gather = [
        Gather(lambda i, p: w_all.at[i, pl.ds(2 * p, 2), pl.ds(0, 4)], x, x_peer),
        Gather(lambda i, p: w_all.at[pl.ds(2 * p, 2), i, pl.ds(4, 4)], y, y_peer),
    ]

    fetch(start_aq, st_b, 4).wait()
    fetch(start_gq, st_s, 5).wait()
    c_gather[0].finish()
    c_gather[1].finish()

    def factor(n, offset, st_ref, e_ref, p_ref):
        count = n // BLK
        where = {pair: position for position, pair in enumerate(PAIRS)}
        squares = jnp.zeros((1, 1), F32)
        for i in range(count):
            for j in range(i, count):
                position = where[(i + offset, j + offset)]
                block = c_blocks[position // 4, position % 4].reshape(BLK, BLK) * (1.0 / SAMPLES)
                for a, b, value in ((i, j, block), (j, i, block.T)) if i != j else ((i, j, block),):
                    at = (slice(a * BLK, (a + 1) * BLK), slice(b * BLK, (b + 1) * BLK))
                    mixed = DECAY * st_ref[at] + (1.0 - DECAY) * value
                    if a == b:
                        mixed = mixed + jnp.where(eye_mask(BLK), DAMPING, 0.0)
                    e_ref[at] = mixed
                    row = jnp.sum(mixed * mixed, axis=0, keepdims=True)
                    squares = squares + jnp.sum(row, axis=1, keepdims=True)
        scale = 1.0 / jnp.sqrt(squares)
        for i in range(count):
            at = slice(i * BLK, (i + 1) * BLK)
            one = jnp.where(row_eye(i, n), 1.0, 0.0)
            rest = one - scale * e_ref[at, :]
            e_ref[at, :] = rest
            p_ref[at, :] = scale * (one + rest)

    factor(BIG, 0, st_b, e_b, p_b)
    g_gather[0].forward()
    g_gather[1].forward()
    factor(SMALL, 4, st_s, e_s, p_s)
    w_gather[0].forward()
    w_gather[1].forward()

    def iterate(step, carry):
        newton_step(BIG, e_b, p_b, eb_b, pb_b)
        newton_step(SMALL, e_s, p_s, eb_s, pb_s)
        return carry

    lax.fori_loop(0, 3, iterate, 0)

    g_gather[0].finish()
    g_gather[1].finish()
    grad = high_low(g_full[...].reshape(BIG, SMALL) * (1.0 / TOKENS))
    for i in range(4):
        at = slice(i * BLK, (i + 1) * BLK)
        m_ref[at, :] = dot3(high_low(p_b[at, :]), grad)
    slot = len(pending)

    w_gather[0].finish()
    w_gather[1].finish()

    @pl.when(core == 0)
    def _():
        def place(step, carry):
            wx, wy = step // 4, lax.rem(step, 4)
            for zh in range(2):
                for cc in range(2):
                    row = pl.multiple_of(((zh * 4 + wx) * 4 + wy) * 16 + cc * 8, 8)
                    for o in range(4):
                        new_q[pl.ds(row, 8), o * 96 : (o + 1) * 96] = w_all[
                            wx, wy, zh * 4 + o, cc, :, 0:96
                        ]
            return carry

        lax.fori_loop(0, 16, place, 0)

    @pl.when(core == 1)
    def _():
        def place(step, carry):
            zh, wx = step // 4, lax.rem(step, 4)
            row = pl.multiple_of(step * 48, 8)
            for o in range(4):
                parts = [
                    w_all[wx, wy, zh * 4 + o, cc, 0:6, :] for wy in range(4) for cc in range(2)
                ]
                new_o[pl.ds(row, 48), o * BLK : (o + 1) * BLK] = jnp.concatenate(parts, axis=0)
            return carry

        lax.fori_loop(0, 8, place, 0)

    def rows_of(ref, i):
        view = ref.at[pl.ds(i * BLK, BLK)]
        return remote(view, view, slot + i, partner)

    @pl.when(core == 0)
    def _():
        right = high_low(p_s[...])
        for i in range(4):
            at = slice(i * BLK, (i + 1) * BLK)
            new_q[at, :] = new_q[at, :] - LEARNING_RATE * dot3(high_low(m_ref[at, :]), right)
            rows_of(new_q, i).start()
        for i in range(4):
            rows_of(new_q, i).wait_send()
        for i in range(3):
            rows_of(new_o, i).wait_recv()

    @pl.when(core == 1)
    def _():
        right = high_low(m_ref[...])
        for i in range(3):
            at = slice(i * BLK, (i + 1) * BLK)
            new_o[at, :] = new_o[at, :] - LEARNING_RATE * dot3(
                high_low(p_s[at, :]), right, ((1,), (1,))
            )
            rows_of(new_o, i).start()
        for i in range(3):
            rows_of(new_o, i).wait_send()
        for i in range(4):
            rows_of(new_q, i).wait_recv()

    for copy in pending:
        copy.wait_send()


COPIES = 128


def per_device(*args):
    hbm = pl.BlockSpec(memory_space=pl.ANY)
    vmem = pl.BlockSpec(memory_space=pltpu.VMEM)
    smem = pl.BlockSpec(memory_space=pltpu.SMEM)

    def v(shape, dtype=F32):
        return pltpu.VMEM(shape, dtype)

    return pl.pallas_call(
        kernel,
        out_shape=(
            jax.ShapeDtypeStruct((BIG, SMALL), F32),
            jax.ShapeDtypeStruct((SMALL, BIG), F32),
        ),
        in_specs=[hbm] * 4 + [smem] + [hbm] * 4 + [vmem] * 2,
        out_specs=(vmem, vmem),
        scratch_shapes=[
            v((1024, BIG), BF16), v((1024, SMALL), BF16), v((1024, BIG), BF16), v((1024, SMALL), BF16),
            v((BIG, BIG)), v((SMALL, SMALL)),
            v((4, BLK, SMALL)), v((4, BLK, SMALL)), v((4, BLK, SMALL)),
            v((2, 4, 2, 2, 16, SMALL)), v((2, 2, 2, 16, SMALL)), v((2, 2, 2, 2, 16, SMALL)),
            v((2, 2, 2, 16, SMALL)), v((2, 4, 16, SMALL)), v((32, SMALL)), v((8, 8, SMALL)),
            v((4, 4, 32, SMALL)),
            v((7, 16, BLK), BF16), v((7, 16, BLK), BF16), v((4, 7, 32, BLK), BF16),
            v((4, 2, 64, BLK)), v((2, 64, BLK)), v((2, 2, 64, BLK)),
            v((BLK, BLK)), v((8, 32, BLK)), v((4, 4, 2, 64, BLK)),
            v((8, BLK)), v((4, 4, 8, 2, 8, BLK)),
            v((BIG, BIG)), v((BIG, BIG)), v((BIG, BIG), BF16), v((BIG, BIG), BF16),
            v((SMALL, SMALL)), v((SMALL, SMALL)), v((SMALL, SMALL), BF16), v((SMALL, SMALL), BF16),
            v((BIG, SMALL)),
            pltpu.SemaphoreType.DMA((6,)),
            pltpu.SemaphoreType.DMA((COPIES,)),
            pltpu.SemaphoreType.DMA((COPIES,)),
        ],
        compiler_params=pltpu.CompilerParams(
            collective_id=0, has_side_effects=True, vmem_limit_bytes=64000000
        ),
    )(*args)


def solution(mesh):
    return jax.shard_map(
        per_device,
        mesh=mesh,
        in_specs=(P(("dp", "own"), None),) * 4
        + (P(("dp", "own")),)
        + (P(),) * 4
        + (P("dp", "own"),) * 2,
        out_specs=(P(), P()),
        check_vma=False,
    )
```

```python
import functools

import jax
import jax.numpy as jnp
from jax import lax
from jax.experimental import pallas as pl
from jax.experimental.pallas import tpu as pltpu
from jax.sharding import PartitionSpec as P

MESH = pl.DeviceIdType.MESH
F32 = jnp.float32
BF16 = jnp.bfloat16
DECAY = 0.5
DAMPING = 0.5
LEARNING_RATE = 10.0
TOKENS = 262144
SAMPLES = 4096
BIG = 512
SMALL = 384
BLK = 128
PAIRS = [(i, j) for i in range(4) for j in range(i, 4)] + [
    (i, j) for i in range(4, 7) for j in range(i, 7)
]


def lookup(index, table):
    value = jnp.int32(table[0])
    for position in range(1, len(table)):
        value = jnp.where(index == position, jnp.int32(table[position]), value)
    return value


def dot(a, b, dims=((1,), (0,))):
    return lax.dot_general(a, b, (dims, ((), ())), preferred_element_type=F32)


def high_low(value):
    high = value.astype(BF16)
    return high, (value - high.astype(F32)).astype(BF16)


def dot3(a, b, dims=((1,), (0,))):
    return dot(a[0], b[0], dims) + dot(a[0], b[1], dims) + dot(a[1], b[0], dims)


def eye_mask(n):
    return lax.broadcasted_iota(jnp.int32, (n, n), 0) == lax.broadcasted_iota(
        jnp.int32, (n, n), 1
    )


def diagonal(ref, n):
    mask = eye_mask(BLK)
    cols, rows = [], []
    for i in range(n // BLK):
        at = slice(i * BLK, (i + 1) * BLK)
        block = jnp.where(mask, ref[at, at], 0.0)
        cols.append(jnp.sum(block, axis=1, keepdims=True))
        rows.append(jnp.sum(block, axis=0, keepdims=True))
    return cols, jnp.concatenate(rows, axis=1)


def row_eye(i, n):
    return lax.broadcasted_iota(jnp.int32, (BLK, n), 0) + i * BLK == lax.broadcasted_iota(
        jnp.int32, (BLK, n), 1
    )


def newton_step(n, e_ref, p_ref, eb_ref, pb_ref):
    blocks = range(n // BLK)
    e_col, e_row = diagonal(e_ref, n)
    for i in blocks:
        at = slice(i * BLK, (i + 1) * BLK)
        eb_ref[at, :] = jnp.where(row_eye(i, n), 0.0, e_ref[at, :]).astype(BF16)
        pb_ref[at, :] = jnp.where(row_eye(i, n), 0.0, p_ref[at, :]).astype(BF16)
    for i in blocks:
        at = slice(i * BLK, (i + 1) * BLK)
        square = dot(eb_ref[at, :], eb_ref[...])
        rest = e_ref[at, :]
        weight = jnp.where(row_eye(i, n), e_col[i], e_col[i] + e_row)
        e_ref[at, :] = square + weight * rest
    f_col, f_row = diagonal(e_ref, n)
    p_col, _ = diagonal(p_ref, n)
    for i in blocks:
        at = slice(i * BLK, (i + 1) * BLK)
        eb_ref[at, :] = jnp.where(row_eye(i, n), 0.0, e_ref[at, :]).astype(BF16)
    for i in blocks:
        at = slice(i * BLK, (i + 1) * BLK)
        product = dot(pb_ref[at, :], eb_ref[...])
        p_rows = p_ref[at, :]
        off = jnp.where(row_eye(i, n), 0.0, e_ref[at, :])
        p_ref[at, :] = p_rows + product + p_col[i] * off + p_rows * f_row


def kernel(
    acts_q, grads_q, acts_o, grads_o, rows_ref,
    start_aq, start_gq, start_ao, start_go, wq_ref, wo_ref,
    new_q, new_o,
    mine_b, mine_s, oth_b, oth_s, st_b, st_s,
    g_send, g_mine, g_core, g_part, g_relay, g_got, g_sum, g_x, g_xsum, g_z, g_full,
    s_send, s_core, s_all,
    c_part, c_relay, c_got, c_ysum, c_z, c_blocks,
    w_send, w_all,
    e_b, p_b, eb_b, pb_b, e_s, p_s, eb_s, pb_s, m_ref,
    in_sem, send_sem, recv_sem,
):
    dp, own = lax.axis_index("dp"), lax.axis_index("own")
    core = lax.rem(dp, 2)
    y = lax.rem(dp // 2, 4)
    x = lax.rem(dp // 8, 4)
    z = (dp // 32) * 4 + own

    def device(cx, cy, cz, cc):
        return ((cz // 4) * 32 + cx * 8 + cy * 2 + cc, lax.rem(cz, 4))

    partner = device(x, y, z, 1 - core)
    x_peer = [device(lax.rem(x + d, 4), y, z, core) for d in range(4)]
    y_peer = [device(x, lax.rem(y + d, 4), z, core) for d in range(4)]
    z_peer = [device(x, y, lax.rem(z + d, 8), core) for d in range(8)]

    def fetch(src, dst, sem):
        return pltpu.make_async_copy(src, dst, in_sem.at[sem])

    @pl.when(core == 0)
    def _():
        fetch(acts_q, mine_b, 0).start()
        fetch(grads_q, mine_s, 1).start()
        fetch(grads_o, oth_b, 2).start()
        fetch(acts_o, oth_s, 3).start()
        fetch(start_aq, st_b, 4).start()
        fetch(start_gq, st_s, 5).start()

    @pl.when(core == 1)
    def _():
        fetch(grads_o, mine_b, 0).start()
        fetch(acts_o, mine_s, 1).start()
        fetch(acts_q, oth_b, 2).start()
        fetch(grads_q, oth_s, 3).start()
        fetch(start_go, st_b, 4).start()
        fetch(start_ao, st_s, 5).start()

    barrier = pltpu.get_barrier_semaphore()
    for peer in [partner] + x_peer[1:] + y_peer[1:] + z_peer[1:]:
        pl.semaphore_signal(barrier, inc=1, device_id=peer, device_id_type=MESH)

    def remote(src, dst, slot, peer):
        return pltpu.make_async_remote_copy(
            src_ref=src, dst_ref=dst, send_sem=send_sem.at[slot],
            recv_sem=recv_sem.at[slot], device_id=peer, device_id_type=MESH,
        )

    pending = []

    def send(src, dst, peer):
        copy = remote(src, dst, len(pending), peer)
        copy.start()
        pending.append(copy)
        return copy

    def land(copies):
        for copy in copies:
            copy.wait_recv()

    def spread(view, peers):
        return [send(view, view, peer) for peer in peers]

    class Scatter:
        def __init__(self, buf, relay, got, me, peer):
            self.buf, self.relay, self.got, self.me, self.peer = buf, relay, got, me, peer
            far, self.after, self.before = (lax.rem(me + d, 4) for d in (2, 1, 3))
            self.first = [
                send(buf.at[far, 0], relay.at[0], peer[1]),
                send(buf.at[far, 1], relay.at[1], peer[3]),
            ]
            self.rest = [
                send(buf.at[self.after, 1], got.at[0, 1], peer[1]),
                send(buf.at[self.before, 0], got.at[1, 0], peer[3]),
            ]

        def forward(self):
            for part, (chunk, peer) in enumerate(((self.after, self.peer[1]), (self.before, self.peer[3]))):
                self.first[part].wait_recv()
                self.buf[chunk, part] = self.buf[chunk, part] + self.relay[part]
                self.rest.append(send(self.buf.at[chunk, part], self.got.at[part, part], peer))

        def sums(self):
            land(self.rest)
            return [(self.buf[self.me, p] + self.got[0, p]) + self.got[1, p] for p in range(2)]

    class Gather:
        def __init__(self, view, me, peer):
            self.view, self.peer = view, peer
            self.after, self.before = lax.rem(me + 1, 4), lax.rem(me + 3, 4)
            mine = [view(me, 0), view(me, 1)]
            self.first = [send(mine[0], mine[0], peer[1]), send(mine[1], mine[1], peer[3])]
            self.rest = [send(mine[1], mine[1], peer[1]), send(mine[0], mine[0], peer[3])]

        def forward(self):
            for part, (chunk, peer) in enumerate(((self.before, self.peer[1]), (self.after, self.peer[3]))):
                self.first[part].wait_recv()
                view = self.view(chunk, part)
                self.rest.append(send(view, view, peer))

        def finish(self):
            land(self.rest)

    w_send[...] = jnp.zeros_like(w_send)

    @pl.when(core == 0)
    def _():
        w_all[x, y, z, 0] = jnp.zeros((8, BLK), F32)
        w_all[x, y, z, 0, :, 0:96] = wq_ref[...]
        w_send[0:6, :] = wo_ref[...]

    @pl.when(core == 1)
    def _():
        w_all[x, y, z, 1] = jnp.zeros((8, BLK), F32)
        w_all[x, y, z, 1, 0:6, :] = wo_ref[...]
        w_send[:, 0:96] = wq_ref[...]

    fetch(acts_q, oth_b, 2).wait()
    fetch(grads_q, oth_s, 3).wait()
    fetch(acts_q, mine_b, 0).wait()
    fetch(grads_q, mine_s, 1).wait()

    target = jnp.zeros((16, 1024), jnp.int32)
    row = lax.broadcasted_iota(jnp.int32, (16, 1024), 0)
    for k in range(16):
        target = jnp.where(row == k, rows_ref[k], target)
    pick = lax.broadcasted_iota(jnp.int32, (16, 1024), 1) == target
    one_hot = jnp.where(pick, 1.0, 0.0).astype(BF16)

    def sampled(big, small):
        return jnp.concatenate([dot(one_hot, big[...]), dot(one_hot, small[...])], axis=1).astype(BF16)

    picked = sampled(oth_b, oth_s)
    for b in range(7):
        s_send[b] = picked[:, b * BLK : (b + 1) * BLK]
    picked = sampled(mine_b, mine_s)
    for b in range(7):
        s_all[x, b, pl.ds(pl.multiple_of(core * 16, 16), 16), :] = picked[:, b * BLK : (b + 1) * BLK]

    pl.semaphore_wait(barrier, 14)

    s_copy = send(s_send, s_core, partner)
    w_copy = send(w_send, w_all.at[x, y, z, core], partner)

    g_copies = []
    for d in (2, 1, 3, 0):
        c = lax.rem(y + d, 4)
        cols = pl.ds(pl.multiple_of(c * BLK, BLK), BLK)
        g_send[d] = dot(oth_b[:, cols], oth_s[...], ((0,), (0,)))
        g_copies.append(send(g_send.at[d], g_core.at[d], partner))
        if d == 2:
            s_copy.wait_recv()
            for b in range(7):
                s_all[x, b, pl.ds(pl.multiple_of((1 - core) * 16, 16), 16), :] = s_core[b]
            s_gather = Gather(lambda i, p: s_all.at[i, pl.ds(4 * p, 4 - p)], x, x_peer)
        g_mine[d] = dot(mine_b[:, cols], mine_s[...], ((0,), (0,)))

    w_copy.wait_recv()
    w_copies = spread(w_all.at[x, y, z], z_peer[1:])
    s_gather.forward()

    for index, d in enumerate((2, 1, 3, 0)):
        c = lax.rem(y + d, 4)
        g_copies[index].wait_recv()
        total = g_mine[d] + g_core[d]
        for b in range(4):
            g_part[0, c, b // 2, b % 2] = total[b * 32 : b * 32 + 16]
            g_part[1, b, c // 2, lax.rem(c, 2)] = total[b * 32 + 16 : b * 32 + 32]
    g_scatter = [
        Scatter(g_part.at[0], g_relay.at[0], g_got.at[0], y, y_peer),
        Scatter(g_part.at[1], g_relay.at[1], g_got.at[1], x, x_peer),
    ]

    s_gather.finish()
    for d in (2, 1, 3, 0):
        c = lax.rem(y + d, 4)
        block = x * 4 + c
        left = lookup(block, [i for i, _ in PAIRS])
        right = lookup(block, [j for _, j in PAIRS])
        lhs = s_all[:, left].reshape(128, BLK)
        rhs = s_all[:, right].reshape(128, BLK)
        value = dot(lhs, rhs, ((0,), (0,)))
        c_part[c, 0] = value[0:64]
        c_part[c, 1] = value[64:128]
    c_scatter = Scatter(c_part, c_relay, c_got, y, y_peer)
    g_scatter[0].forward()
    g_scatter[1].forward()
    c_scatter.forward()

    for p, value in enumerate(c_scatter.sums()):
        c_ysum[p * 64 : (p + 1) * 64, :] = value
    cz_copies = []
    for d in range(1, 8):
        rows = pl.ds(pl.multiple_of(lax.rem(z + d, 4) * 32, 32), 32)
        cz_copies.append(send(c_ysum.at[rows], c_z.at[z], z_peer[d]))
    c_z[z] = c_ysum[pl.ds(pl.multiple_of(own * 32, 32), 32), :]

    for h in range(2):
        for p, value in enumerate(g_scatter[h].sums()):
            g_sum[h, p] = value
    gx_copies = []
    for d in (1, 2, 3):
        to = lax.rem(x + d, 4)
        gx_copies.append(send(g_sum.at[0, to // 2, lax.rem(to, 2)], g_x.at[0, x], x_peer[d]))
        to = lax.rem(y + d, 4)
        gx_copies.append(send(g_sum.at[1, to // 2, lax.rem(to, 2)], g_x.at[1, y], y_peer[d]))
    g_x[0, x] = g_sum[0, x // 2, lax.rem(x, 2)]
    g_x[1, y] = g_sum[1, y // 2, lax.rem(y, 2)]

    land(w_copies)
    w_copies = spread(w_all.at[x, y, pl.ds(0, 4)], y_peer[1:])
    w_copies += spread(w_all.at[x, y, pl.ds(4, 4)], x_peer[1:])

    land(gx_copies)
    for h in range(2):
        g_xsum[h * 16 : (h + 1) * 16, :] = (g_x[h, 0] + g_x[h, 1]) + (g_x[h, 2] + g_x[h, 3])
    gz_copies = []
    for d in range(1, 8):
        rows = pl.ds(pl.multiple_of(lax.rem(z + d, 4) * 8, 8), 8)
        gz_copies.append(send(g_xsum.at[rows], g_z.at[z], z_peer[d]))
    g_z[z] = g_xsum[pl.ds(pl.multiple_of(own * 8, 8), 8), :]

    land(w_copies)
    w_gather = [
        Gather(lambda i, p: w_all.at[i, pl.ds(2 * p, 2), pl.ds(0, 4)], x, x_peer),
        Gather(lambda i, p: w_all.at[pl.ds(2 * p, 2), i, pl.ds(4, 4)], y, y_peer),
    ]

    land(cz_copies)
    total = c_z[0]
    for k in range(1, 8):
        total = total + c_z[k]
    c_view = (x, y, own // 2, pl.ds(pl.multiple_of(lax.rem(own, 2) * 32, 32), 32))
    c_blocks[c_view] = total
    cag_copies = spread(c_blocks.at[c_view], [z_peer[d] for d in (1, 7, 6)])

    w_gather[0].forward()
    w_gather[1].forward()

    land(cag_copies)
    cag_copies = spread(c_blocks.at[x, y, 0], y_peer[1:]) + spread(c_blocks.at[x, y, 1], x_peer[1:])

    land(gz_copies)
    total = g_z[0]
    for k in range(1, 8):
        total = total + g_z[k]
    g_view = (y, x, pl.ds(pl.multiple_of(own * 8, 8), 8))
    g_full[g_view] = total
    gag_copies = spread(g_full.at[g_view], [z_peer[d] for d in (1, 7, 6)])

    land(cag_copies)
    c_gather = [
        Gather(lambda i, p: c_blocks.at[i, pl.ds(2 * p, 2), 0], x, x_peer),
        Gather(lambda i, p: c_blocks.at[pl.ds(2 * p, 2), i, 1], y, y_peer),
    ]

    land(gag_copies)
    gag_copies = spread(g_full.at[y, x, pl.ds(0, 16)], x_peer[1:])
    gag_copies += spread(g_full.at[y, x, pl.ds(16, 16)], y_peer[1:])
    c_gather[0].forward()
    c_gather[1].forward()
    land(gag_copies)
    g_gather = [
        Gather(lambda i, p: g_full.at[i, pl.ds(2 * p, 2), pl.ds(0, 16)], y, y_peer),
        Gather(lambda i, p: g_full.at[pl.ds(2 * p, 2), i, pl.ds(16, 16)], x, x_peer),
    ]

    w_gather[0].finish()
    w_gather[1].finish()

    @pl.when(core == 0)
    def _():
        def place(step, carry):
            wx, wy = step // 4, lax.rem(step, 4)
            for zh in range(2):
                for cc in range(2):
                    row = pl.multiple_of(((zh * 4 + wx) * 4 + wy) * 16 + cc * 8, 8)
                    for o in range(4):
                        new_q[pl.ds(row, 8), o * 96 : (o + 1) * 96] = w_all[
                            wx, wy, zh * 4 + o, cc, :, 0:96
                        ]
            return carry

        lax.fori_loop(0, 16, place, 0)

    @pl.when(core == 1)
    def _():
        def place(step, carry):
            zh, wx = step // 4, lax.rem(step, 4)
            row = pl.multiple_of(step * 48, 8)
            for o in range(4):
                parts = [
                    w_all[wx, wy, zh * 4 + o, cc, 0:6, :] for wy in range(4) for cc in range(2)
                ]
                new_o[pl.ds(row, 48), o * BLK : (o + 1) * BLK] = jnp.concatenate(parts, axis=0)
            return carry

        lax.fori_loop(0, 8, place, 0)

    fetch(start_aq, st_b, 4).wait()
    fetch(start_gq, st_s, 5).wait()
    c_gather[0].finish()
    c_gather[1].finish()

    def factor(n, offset, st_ref, e_ref, p_ref):
        count = n // BLK
        where = {pair: position for position, pair in enumerate(PAIRS)}
        squares = jnp.zeros((1, 1), F32)
        for i in range(count):
            for j in range(i, count):
                position = where[(i + offset, j + offset)]
                block = c_blocks[position // 4, position % 4].reshape(BLK, BLK) * (1.0 / SAMPLES)
                for a, b, value in ((i, j, block), (j, i, block.T)) if i != j else ((i, j, block),):
                    at = (slice(a * BLK, (a + 1) * BLK), slice(b * BLK, (b + 1) * BLK))
                    mixed = DECAY * st_ref[at] + (1.0 - DECAY) * value
                    if a == b:
                        mixed = mixed + jnp.where(eye_mask(BLK), DAMPING, 0.0)
                    e_ref[at] = mixed
                    row = jnp.sum(mixed * mixed, axis=0, keepdims=True)
                    squares = squares + jnp.sum(row, axis=1, keepdims=True)
        scale = 1.0 / jnp.sqrt(squares)
        for i in range(count):
            at = slice(i * BLK, (i + 1) * BLK)
            one = jnp.where(row_eye(i, n), 1.0, 0.0)
            rest = one - scale * e_ref[at, :]
            e_ref[at, :] = rest
            p_ref[at, :] = scale * (one + rest)

    factor(BIG, 0, st_b, e_b, p_b)
    g_gather[0].forward()
    g_gather[1].forward()
    factor(SMALL, 4, st_s, e_s, p_s)

    def iterate(step, carry):
        newton_step(BIG, e_b, p_b, eb_b, pb_b)
        newton_step(SMALL, e_s, p_s, eb_s, pb_s)
        return carry

    lax.fori_loop(0, 3, iterate, 0)

    g_gather[0].finish()
    g_gather[1].finish()
    grad = high_low(g_full[...].reshape(BIG, SMALL) * (1.0 / TOKENS))
    for i in range(4):
        at = slice(i * BLK, (i + 1) * BLK)
        m_ref[at, :] = dot3(high_low(p_b[at, :]), grad)
    slot = len(pending)

    def rows_of(ref, i):
        view = ref.at[pl.ds(i * BLK, BLK)]
        return remote(view, view, slot + i, partner)

    @pl.when(core == 0)
    def _():
        right = high_low(p_s[...])
        for i in range(4):
            at = slice(i * BLK, (i + 1) * BLK)
            new_q[at, :] = new_q[at, :] - LEARNING_RATE * dot3(high_low(m_ref[at, :]), right)
            rows_of(new_q, i).start()
        for i in range(4):
            rows_of(new_q, i).wait_send()
        for i in range(3):
            rows_of(new_o, i).wait_recv()

    @pl.when(core == 1)
    def _():
        right = high_low(m_ref[...])
        for i in range(3):
            at = slice(i * BLK, (i + 1) * BLK)
            new_o[at, :] = new_o[at, :] - LEARNING_RATE * dot3(
                high_low(p_s[at, :]), right, ((1,), (1,))
            )
            rows_of(new_o, i).start()
        for i in range(3):
            rows_of(new_o, i).wait_send()
        for i in range(4):
            rows_of(new_q, i).wait_recv()

    for copy in pending:
        copy.wait_send()


COPIES = 128


def per_device(*args):
    hbm = pl.BlockSpec(memory_space=pl.ANY)
    vmem = pl.BlockSpec(memory_space=pltpu.VMEM)
    smem = pl.BlockSpec(memory_space=pltpu.SMEM)

    def v(shape, dtype=F32):
        return pltpu.VMEM(shape, dtype)

    return pl.pallas_call(
        kernel,
        out_shape=(
            jax.ShapeDtypeStruct((BIG, SMALL), F32),
            jax.ShapeDtypeStruct((SMALL, BIG), F32),
        ),
        in_specs=[hbm] * 4 + [smem] + [hbm] * 4 + [vmem] * 2,
        out_specs=(vmem, vmem),
        scratch_shapes=[
            v((1024, BIG), BF16), v((1024, SMALL), BF16), v((1024, BIG), BF16), v((1024, SMALL), BF16),
            v((BIG, BIG)), v((SMALL, SMALL)),
            v((4, BLK, SMALL)), v((4, BLK, SMALL)), v((4, BLK, SMALL)),
            v((2, 4, 2, 2, 16, SMALL)), v((2, 2, 2, 16, SMALL)), v((2, 2, 2, 2, 16, SMALL)),
            v((2, 2, 2, 16, SMALL)), v((2, 4, 16, SMALL)), v((32, SMALL)), v((8, 8, SMALL)),
            v((4, 4, 32, SMALL)),
            v((7, 16, BLK), BF16), v((7, 16, BLK), BF16), v((4, 7, 32, BLK), BF16),
            v((4, 2, 64, BLK)), v((2, 64, BLK)), v((2, 2, 64, BLK)),
            v((BLK, BLK)), v((8, 32, BLK)), v((4, 4, 2, 64, BLK)),
            v((8, BLK)), v((4, 4, 8, 2, 8, BLK)),
            v((BIG, BIG)), v((BIG, BIG)), v((BIG, BIG), BF16), v((BIG, BIG), BF16),
            v((SMALL, SMALL)), v((SMALL, SMALL)), v((SMALL, SMALL), BF16), v((SMALL, SMALL), BF16),
            v((BIG, SMALL)),
            pltpu.SemaphoreType.DMA((6,)),
            pltpu.SemaphoreType.DMA((COPIES,)),
            pltpu.SemaphoreType.DMA((COPIES,)),
        ],
        compiler_params=pltpu.CompilerParams(
            collective_id=0, has_side_effects=True, vmem_limit_bytes=64000000
        ),
    )(*args)


def solution(mesh):
    return jax.shard_map(
        per_device,
        mesh=mesh,
        in_specs=(P(("dp", "own"), None),) * 4
        + (P(("dp", "own")),)
        + (P(),) * 4
        + (P("dp", "own"),) * 2,
        out_specs=(P(), P()),
        check_vma=False,
    )
```
